32 devices in a mesh: row: 8 (over y, x, core), col: 4 (over z).
Axes of the slice: x: 2, y: 2, z: 4, core: 2. Of those that a mesh axis runs over, the one named last changes fastest.
Arguments:
- panel_rows: float32 [128, 1024], P('row', 'col'), may hold values from 0.1 to 10
- trans_bias: float32 [12288, 128], P('row'), may hold values from 0.002 to 0.05
- trans_rate: float32 [1024, 512], P('col'), may hold values from 0.0005 to 0.01
- likelihood: float32 [12288, 1024], P('row', 'col'), may hold values from 0.1 to 720
Outputs:
- posterior: float32 [12288, 1024], P('row', 'col')
The draws below stay inside these ranges and needn't reach their ends.
All inputs are finite; a program needn't handle non-finite values.
Results may differ from the reference program's by a relative error of at most 0.00005.
Values sent between devices are 32-bit elements; how exact they have to be, the bound alone decides.
A program may use at most 64 MiB of HBM per device.

```python
import math
import jax
import jax.numpy as jnp
from jax import lax

RATE_DEV = 256
PANEL = 64
NB = 12288
NR = 1024
N_COL = 4


def draw_likelihood(key, part):
    noise_key = jax.random.fold_in(key, 0)
    roughness = jnp.exp(jax.random.uniform(noise_key, (NB, NR), jnp.float32, jnp.log(0.1), jnp.log(10.0)))
    position = jnp.arange(NB, dtype=jnp.float32) / float(max(NB - 1, 1))
    rising = jnp.exp(jnp.log(3.0) * position)
    return (roughness * rising[:, None]).astype(jnp.float32)


def level_of(own_key, extent, cuts, smallest, high):
    level = 1.0
    for dim, blocks in cuts:
        heights = jax.random.uniform(jax.random.fold_in(jax.random.fold_in(own_key, 6), dim), (blocks,), jnp.float32, smallest / len(cuts), high / len(cuts))
        level = level * jnp.repeat(jnp.exp(heights), extent[dim] // blocks).reshape((-1,) + (1,) * (len(extent) - 1 - dim))
    return level


def setup_inputs(seed: int = 0) -> dict:
    key_of = jax.random.split(jax.random.key(seed), 5)
    return {
        "panel_rows": jnp.clip(jnp.exp(math.log(10.0) - 4.6051702 * jax.random.uniform(key_of[0], (2 * PANEL, NR), jnp.float32) ** level_of(key_of[0], (2 * PANEL, NR), ((0, 8), (1, 4)), -0.2, 0.2)), 0.1, 10.0),
        "trans_bias": jnp.clip(jnp.exp(math.log(0.05) - 3.218876 * jax.random.uniform(key_of[1], (NB, 2 * PANEL), jnp.float32) ** level_of(key_of[1], (NB, 2 * PANEL), ((0, 8),), -0.2, 0.2)), 0.002, 0.05),
        "trans_rate": jnp.clip(jnp.exp(math.log(0.01) - 2.9957322 * jax.random.uniform(key_of[2], (NR, 2 * RATE_DEV), jnp.float32) ** level_of(key_of[2], (NR, 2 * RATE_DEV), ((0, 4),), -0.2, 0.2)), 0.0005, 0.01),
        "likelihood": draw_likelihood(jax.random.fold_in(key_of[4], 71), 0),
    }


def reference(panel_rows, trans_bias, trans_rate, likelihood):
    highest = lax.Precision.HIGHEST
    prior = jnp.dot(trans_bias, panel_rows, precision=highest, preferred_element_type=jnp.float32)
    blocks = prior.reshape(NB, N_COL, RATE_DEV)
    following = jnp.roll(blocks, -1, axis=1)
    rate_blocks = trans_rate.reshape(N_COL, RATE_DEV, 2 * RATE_DEV)
    predicted = jnp.einsum("bjc,jrc->bjr", blocks, rate_blocks[:, :, :RATE_DEV], precision=highest)
    predicted = predicted + jnp.einsum("bjc,jrc->bjr", following, rate_blocks[:, :, RATE_DEV:], precision=highest)
    predicted = predicted.reshape(NB, NR)
    weighted = likelihood * predicted
    total_mass = jnp.sum(weighted)
    return weighted * (float(NB * NR) / total_mass)
```

```python
import functools

import jax
import jax.numpy as jnp
from jax import lax
from jax.experimental import pallas as pl
from jax.experimental.pallas import tpu as pltpu
from jax.sharding import PartitionSpec as P

MESH = pl.DeviceIdType.MESH
HIGHEST = lax.Precision.HIGHEST
F32 = jnp.float32


def dot(a, b, contract):
    return lax.dot_general(
        a, b, ((contract[:1], contract[1:]), ((), ())),
        precision=HIGHEST, preferred_element_type=F32,
    )


def window_kernel(
    n_row, n_col, cells,
    p_hbm, t_hbm, r_hbm, l_hbm,
    w_ref, s_ref,
    p_buf, p_next, t_buf, r_buf, l_buf, g_out, g_in, m_buf, mass_out, mass_in,
    load_sems, p_send, p_recv, g_send, g_recv, m_send, m_recv, mass_send, mass_recv,
):
    i = lax.axis_index("row")
    j = lax.axis_index("col")
    rows, width = p_buf.shape
    n = n_row * n_col
    loads = [
        pltpu.make_async_copy(src, dst, load_sems.at[k])
        for k, (src, dst) in enumerate(
            [(t_hbm, t_buf), (l_hbm, l_buf), (p_hbm, p_buf), (r_hbm, r_buf)]
        )
    ]
    for load in loads:
        load.start()

    barrier = pltpu.get_barrier_semaphore()
    for d in range(1, n_row):
        pl.semaphore_signal(
            barrier, inc=1, device_id=(lax.rem(i + d, n_row), j), device_id_type=MESH
        )
    for d in range(1, n_col):
        pl.semaphore_signal(
            barrier, inc=1, device_id=(i, lax.rem(j + d, n_col)), device_id_type=MESH
        )
    pl.semaphore_wait(barrier, n_row - 1 + n_col - 1)

    next_copy = pltpu.make_async_remote_copy(
        src_ref=p_hbm, dst_ref=p_next, send_sem=p_send, recv_sem=p_recv,
        device_id=(i, lax.rem(j + n_col - 1, n_col)), device_id_type=MESH,
    )
    next_copy.start()

    loads[0].wait()
    loads[1].wait()
    g = dot(t_buf[...], l_buf[...], (0, 0))
    for q in range(n_row):
        g_out[q] = g[q * rows:(q + 1) * rows]
    for d in range(1, n_row):
        peer = lax.rem(i + d, n_row)
        pltpu.make_async_remote_copy(
            src_ref=g_out.at[peer], dst_ref=g_in.at[d - 1],
            send_sem=g_send, recv_sem=g_recv,
            device_id=(peer, j), device_id_type=MESH,
        ).start()

    loads[2].wait()
    loads[3].wait()
    m = dot(p_buf[...], r_buf[:, :width], (1, 1))
    next_copy.wait()
    m = m + dot(p_next[...], r_buf[:, width:], (1, 1))
    m_buf[i] = m
    for d in range(1, n_row):
        pltpu.make_async_remote_copy(
            src_ref=m_buf.at[i], dst_ref=m_buf.at[i],
            send_sem=m_send, recv_sem=m_recv,
            device_id=(lax.rem(i + d, n_row), j), device_id_type=MESH,
        ).start()

    pltpu.make_async_copy(g_in, g_in, g_recv).wait()
    g_sum = g_out[i]
    for d in range(1, n_row):
        g_sum = g_sum + g_in[d - 1]
    mass = jnp.sum(g_sum * m, axis=0, keepdims=True)
    mass = sum(mass[:, k:k + 128] for k in range(0, width, 128))
    mass_out[...] = mass
    me = i * n_col + j

    def send_mass(d, carry):
        peer = lax.rem(me + d, n)
        pltpu.make_async_remote_copy(
            src_ref=mass_out, dst_ref=mass_in.at[d - 1],
            send_sem=mass_send, recv_sem=mass_recv,
            device_id=(peer // n_col, lax.rem(peer, n_col)), device_id_type=MESH,
        ).start()
        return carry

    lax.fori_loop(1, n, send_mass, 0)

    others = m_buf.at[pl.ds(0, n_row - 1)]
    pltpu.make_async_copy(others, others, m_recv).wait()
    m_all = jnp.concatenate([m_buf[q] for q in range(n_row)], axis=0)
    w_ref[...] = l_buf[...] * dot(t_buf[...], m_all, (1, 0))

    pltpu.make_async_copy(mass_in, mass_in, mass_recv).wait()
    total = jnp.sum(mass + jnp.sum(mass_in[...], axis=0))
    s_ref[...] = jnp.full(s_ref.shape, cells, F32) / total

    pltpu.make_async_copy(g_in, g_in, g_send).wait()
    pltpu.make_async_copy(others, others, m_send).wait()
    pltpu.make_async_copy(mass_in, mass_in, mass_send).wait()


def shards(panel_rows, trans_bias, trans_rate, likelihood):
    n_row, n_col = lax.axis_size("row"), lax.axis_size("col")
    rows, width = panel_rows.shape
    cells = float(likelihood.shape[0] * n_row * likelihood.shape[1] * n_col)
    dma = pltpu.SemaphoreType.DMA
    weighted, scale = pl.pallas_call(
        functools.partial(window_kernel, n_row, n_col, cells),
        out_shape=(
            jax.ShapeDtypeStruct(likelihood.shape, F32),
            jax.ShapeDtypeStruct((1, 128), F32),
        ),
        in_specs=[pl.BlockSpec(memory_space=pl.ANY)] * 4,
        out_specs=(
            pl.BlockSpec(memory_space=pltpu.VMEM),
            pl.BlockSpec(memory_space=pltpu.VMEM),
        ),
        scratch_shapes=[
            pltpu.VMEM((rows, width), F32),
            pltpu.VMEM((rows, width), F32),
            pltpu.VMEM(trans_bias.shape, F32),
            pltpu.VMEM(trans_rate.shape, F32),
            pltpu.VMEM(likelihood.shape, F32),
            pltpu.VMEM((n_row, rows, width), F32),
            pltpu.VMEM((n_row - 1, rows, width), F32),
            pltpu.VMEM((n_row, rows, width), F32),
            pltpu.VMEM((1, 128), F32),
            pltpu.VMEM((n_row * n_col - 1, 1, 128), F32),
            dma((4,)), dma, dma, dma, dma, dma, dma, dma, dma,
        ],
        compiler_params=pltpu.CompilerParams(collective_id=0, has_side_effects=True, vmem_limit_bytes=24 * 2**20),
        name="window",
    )(panel_rows, trans_bias, trans_rate, likelihood)
    return weighted * scale[0, 0]


def solution(mesh):
    placed = (P("row", "col"), P("row", None), P("col", None), P("row", "col"))
    return jax.shard_map(
        shards, mesh=mesh, in_specs=placed, out_specs=P("row", "col"), check_vma=False
    )
```

```python
import functools

import jax
import jax.numpy as jnp
from jax import lax
from jax.experimental import pallas as pl
from jax.experimental.pallas import tpu as pltpu
from jax.sharding import PartitionSpec as P

MESH = pl.DeviceIdType.MESH
F32 = jnp.float32


def split(x):
    high = x.astype(jnp.bfloat16)
    return high, (x - high.astype(F32)).astype(jnp.bfloat16)


def dot_bf16(a, b, contract):
    return lax.dot_general(
        a, b, ((contract[:1], contract[1:]), ((), ())), preferred_element_type=F32
    )


def wrapped(position, size):
    return jnp.where(position >= size, position - size, position)


def window_kernel(
    n_row, n_col, cells,
    p_hbm, t_hbm, r_hbm, l_hbm,
    w_ref, s_ref,
    p_buf, p_next, t_buf, t_parts, r_buf, r_parts, l_buf, g_out, g_in, m_buf, mass_out, mass_in,
    load_sems, p_send, p_recv, g_send, g_recv, m_send, m_recv, mass_send, mass_recv,
):
    i = lax.axis_index("row")
    j = lax.axis_index("col")
    rows, width = p_buf.shape
    row_of = [i] + [wrapped(i + d, n_row) for d in range(1, n_row)]
    col_of = [j] + [wrapped(j + d, n_col) for d in range(1, n_col)]
    loads = [
        pltpu.make_async_copy(src, dst, load_sems.at[k])
        for k, (src, dst) in enumerate(
            [(t_hbm, t_buf), (l_hbm, l_buf), (p_hbm, p_buf), (r_hbm, r_buf)]
        )
    ]
    for load in loads:
        load.start()

    barrier = pltpu.get_barrier_semaphore()
    for d in range(1, n_row):
        pl.semaphore_signal(
            barrier, inc=1, device_id=(row_of[d], j), device_id_type=MESH
        )
    for d in range(1, n_col):
        pl.semaphore_signal(
            barrier, inc=1, device_id=(i, col_of[d]), device_id_type=MESH
        )
    loads[0].wait()
    loads[1].wait()
    depth = t_buf.shape[1]
    t_high, t_low = split(t_buf[...])
    t_parts[:, :depth] = t_high
    t_parts[:, depth:] = t_low
    l_high, l_low = split(l_buf[...])
    g = dot_bf16(t_parts[...], l_high, (0, 0))
    g = g[:depth] + g[depth:] + dot_bf16(t_parts[:, :depth], l_low, (0, 0))
    for q in range(n_row):
        g_out[q] = g[q * rows:(q + 1) * rows]
    pl.semaphore_wait(barrier, n_row - 1 + n_col - 1)

    next_copy = pltpu.make_async_remote_copy(
        src_ref=p_hbm, dst_ref=p_next, send_sem=p_send, recv_sem=p_recv,
        device_id=(i, col_of[n_col - 1]), device_id_type=MESH,
    )
    next_copy.start()

    for d in range(1, n_row):
        peer = row_of[d]
        pltpu.make_async_remote_copy(
            src_ref=g_out.at[peer], dst_ref=g_in.at[d - 1],
            send_sem=g_send, recv_sem=g_recv,
            device_id=(peer, j), device_id_type=MESH,
        ).start()

    loads[2].wait()
    loads[3].wait()
    r_high, r_low = split(r_buf[...].T)
    r_parts[0] = r_high
    r_parts[1] = r_low

    def rate_rows(p_rows, start):
        p_high, p_low = split(p_rows)
        high = r_parts[0, start:start + width]
        low = r_parts[1, start:start + width]
        return (
            dot_bf16(p_high, low, (1, 0)) + dot_bf16(p_low, high, (1, 0))
            + dot_bf16(p_high, high, (1, 0))
        )

    m = rate_rows(p_buf[...], 0)
    next_copy.wait()
    m = m + rate_rows(p_next[...], width)
    m_buf[i] = m
    for d in range(1, n_row):
        pltpu.make_async_remote_copy(
            src_ref=m_buf.at[i], dst_ref=m_buf.at[i],
            send_sem=m_send, recv_sem=m_recv,
            device_id=(row_of[d], j), device_id_type=MESH,
        ).start()

    pltpu.make_async_copy(g_in, g_in, g_recv).wait()
    g_sum = g_out[i]
    for d in range(1, n_row):
        g_sum = g_sum + g_in[d - 1]
    mass = jnp.sum(g_sum * m, axis=0, keepdims=True)
    mass = sum(mass[:, k:k + 128] for k in range(0, width, 128))
    mass_out[...] = mass

    def send_mass(row, first, from_col):
        for d in range(from_col, n_col):
            pltpu.make_async_remote_copy(
                src_ref=mass_out, dst_ref=mass_in.at[first + d - 1],
                send_sem=mass_send, recv_sem=mass_recv,
                device_id=(row, col_of[d]), device_id_type=MESH,
            ).start()

    if n_row * n_col <= 64:
        for d in reversed(range(1, n_row)):
            send_mass(row_of[d], d * n_col, 0)
    else:

        def send_row(d, carry):
            send_mass(wrapped(i + d, n_row), d * n_col, 0)
            return carry

        lax.fori_loop(1, n_row, send_row, 0)
    send_mass(i, 0, 1)

    others = m_buf.at[pl.ds(0, n_row - 1)]
    pltpu.make_async_copy(others, others, m_recv).wait()
    m_all = jnp.concatenate([m_buf[q] for q in range(n_row)], axis=0)
    m_high, m_low = split(m_all)
    predicted = dot_bf16(t_parts[...], jnp.concatenate([m_high, m_high], axis=0), (1, 0))
    predicted = predicted + dot_bf16(t_parts[:, :depth], m_low, (1, 0))
    w_ref[...] = l_buf[...] * predicted

    pltpu.make_async_copy(mass_in, mass_in, mass_recv).wait()
    total = jnp.sum(mass + jnp.sum(mass_in[...], axis=0))
    s_ref[...] = jnp.full(s_ref.shape, cells, F32) / total

    pltpu.make_async_copy(g_in, g_in, g_send).wait()
    pltpu.make_async_copy(others, others, m_send).wait()
    pltpu.make_async_copy(mass_in, mass_in, mass_send).wait()


def shards(panel_rows, trans_bias, trans_rate, likelihood):
    n_row, n_col = lax.axis_size("row"), lax.axis_size("col")
    rows, width = panel_rows.shape
    cells = float(likelihood.shape[0] * n_row * likelihood.shape[1] * n_col)
    dma = pltpu.SemaphoreType.DMA
    weighted, scale = pl.pallas_call(
        functools.partial(window_kernel, n_row, n_col, cells),
        out_shape=(
            jax.ShapeDtypeStruct(likelihood.shape, F32),
            jax.ShapeDtypeStruct((1, 128), F32),
        ),
        in_specs=[pl.BlockSpec(memory_space=pltpu.HBM)] * 4,
        out_specs=(
            pl.BlockSpec(memory_space=pltpu.VMEM),
            pl.BlockSpec(memory_space=pltpu.VMEM),
        ),
        scratch_shapes=[
            pltpu.VMEM((rows, width), F32),
            pltpu.VMEM((rows, width), F32),
            pltpu.VMEM(trans_bias.shape, F32),
            pltpu.VMEM((trans_bias.shape[0], 2 * trans_bias.shape[1]), jnp.bfloat16),
            pltpu.VMEM(trans_rate.shape, F32),
            pltpu.VMEM((2,) + trans_rate.shape[::-1], jnp.bfloat16),
            pltpu.VMEM(likelihood.shape, F32),
            pltpu.VMEM((n_row, rows, width), F32),
            pltpu.VMEM((n_row - 1, rows, width), F32),
            pltpu.VMEM((n_row, rows, width), F32),
            pltpu.VMEM((1, 128), F32),
            pltpu.VMEM((n_row * n_col - 1, 1, 128), F32),
            dma((4,)), dma, dma, dma, dma, dma, dma, dma, dma,
        ],
        compiler_params=pltpu.CompilerParams(collective_id=0, has_side_effects=True, vmem_limit_bytes=24 * 2**20),
        name="window",
    )(*[pltpu.with_memory_space_constraint(x, pltpu.HBM) for x in (panel_rows, trans_bias, trans_rate, likelihood)])
    return weighted * scale[0, 0]


def solution(mesh):
    placed = (P("row", "col"), P("row", None), P("col", None), P("row", "col"))
    return jax.shard_map(
        shards, mesh=mesh, in_specs=placed, out_specs=P("row", "col"), check_vma=False
    )
```

```python
import functools

import jax
import jax.numpy as jnp
from jax import lax
from jax.experimental import pallas as pl
from jax.experimental.pallas import tpu as pltpu
from jax.sharding import PartitionSpec as P

MESH = pl.DeviceIdType.MESH
F32 = jnp.float32
PIECES = 1


def split(x):
    high = x.astype(jnp.bfloat16)
    return high, (x - high.astype(F32)).astype(jnp.bfloat16)


def dot_bf16(a, b, contract):
    return lax.dot_general(
        a, b, ((contract[:1], contract[1:]), ((), ())), preferred_element_type=F32
    )


def wrapped(position, size):
    return jnp.where(position >= size, position - size, position)


def window_kernel(
    n_row, n_col, cells,
    p_hbm, t_hbm, r_hbm, l_hbm,
    w_ref, s_ref,
    p_buf, p_next, t_buf, t_parts, r_buf, r_parts, l_buf, g_out, g_in, m_buf, mass_out, mass_in,
    load_sems, p_send, p_recv, g_send, g_recv, m_send, m_recv, mass_send, mass_recv,
):
    i = lax.axis_index("row")
    j = lax.axis_index("col")
    rows, width = p_buf.shape
    row_of = [i] + [wrapped(i + d, n_row) for d in range(1, n_row)]
    col_of = [j] + [wrapped(j + d, n_col) for d in range(1, n_col)]
    depth = t_buf.shape[1]
    height = t_buf.shape[0] // PIECES
    pieces = [pl.ds(k * height, height) for k in range(PIECES)]
    p_load = pltpu.make_async_copy(p_hbm, p_buf, load_sems.at[0])
    r_load = pltpu.make_async_copy(r_hbm, r_buf, load_sems.at[1])
    t_loads = [
        pltpu.make_async_copy(t_hbm.at[piece], t_buf.at[piece], load_sems.at[2 + k])
        for k, piece in enumerate(pieces)
    ]
    l_loads = [
        pltpu.make_async_copy(l_hbm.at[piece], l_buf.at[piece], load_sems.at[2 + PIECES + k])
        for k, piece in enumerate(pieces)
    ]
    p_load.start()
    for t_load, l_load in zip(t_loads, l_loads):
        t_load.start()
        l_load.start()
    r_load.start()

    barrier = pltpu.get_barrier_semaphore()
    for d in range(1, n_row):
        pl.semaphore_signal(
            barrier, inc=1, device_id=(row_of[d], j), device_id_type=MESH
        )
    for d in range(1, n_col):
        pl.semaphore_signal(
            barrier, inc=1, device_id=(i, col_of[d]), device_id_type=MESH
        )
    g = None
    for piece, t_load, l_load in zip(pieces, t_loads, l_loads):
        t_load.wait()
        t_high, t_low = split(t_buf[piece])
        t_parts[piece, :depth] = t_high
        t_parts[piece, depth:] = t_low
        l_load.wait()
        l_high, l_low = split(l_buf[piece])
        both = dot_bf16(t_parts[piece], l_high, (0, 0))
        part = both[:depth] + both[depth:] + dot_bf16(t_high, l_low, (0, 0))
        g = part if g is None else g + part
    for q in range(n_row):
        g_out[q] = g[q * rows:(q + 1) * rows]
    p_load.wait()
    r_load.wait()
    r_high, r_low = split(r_buf[...].T)
    r_parts[0] = r_high
    r_parts[1] = r_low

    def rate_rows(p_rows, start):
        p_high, p_low = split(p_rows)
        high = r_parts[0, start:start + width]
        low = r_parts[1, start:start + width]
        return (
            dot_bf16(p_high, low, (1, 0)) + dot_bf16(p_low, high, (1, 0))
            + dot_bf16(p_high, high, (1, 0))
        )

    m = rate_rows(p_buf[...], 0)
    pl.semaphore_wait(barrier, n_row - 1 + n_col - 1)

    next_copy = pltpu.make_async_remote_copy(
        src_ref=p_buf, dst_ref=p_next, send_sem=p_send, recv_sem=p_recv,
        device_id=(i, col_of[n_col - 1]), device_id_type=MESH,
    )
    next_copy.start()

    for d in range(1, n_row):
        peer = row_of[d]
        pltpu.make_async_remote_copy(
            src_ref=g_out.at[peer], dst_ref=g_in.at[d - 1],
            send_sem=g_send, recv_sem=g_recv,
            device_id=(peer, j), device_id_type=MESH,
        ).start()

    next_copy.wait()
    m = m + rate_rows(p_next[...], width)
    m_buf[i] = m
    for d in range(1, n_row):
        pltpu.make_async_remote_copy(
            src_ref=m_buf.at[i], dst_ref=m_buf.at[i],
            send_sem=m_send, recv_sem=m_recv,
            device_id=(row_of[d], j), device_id_type=MESH,
        ).start()

    pltpu.make_async_copy(g_in, g_in, g_recv).wait()
    g_sum = g_out[i]
    for d in range(1, n_row):
        g_sum = g_sum + g_in[d - 1]
    mass = jnp.sum(g_sum * m, axis=0, keepdims=True)
    mass = sum(mass[:, k:k + 128] for k in range(0, width, 128))
    mass_out[...] = mass

    def send_mass(row, first, from_col):
        for d in range(from_col, n_col):
            pltpu.make_async_remote_copy(
                src_ref=mass_out, dst_ref=mass_in.at[first + d - 1],
                send_sem=mass_send, recv_sem=mass_recv,
                device_id=(row, col_of[d]), device_id_type=MESH,
            ).start()

    if n_row * n_col <= 64:
        for d in reversed(range(1, n_row)):
            send_mass(row_of[d], d * n_col, 0)
    else:

        def send_row(d, carry):
            send_mass(wrapped(i + d, n_row), d * n_col, 0)
            return carry

        lax.fori_loop(1, n_row, send_row, 0)
    send_mass(i, 0, 1)

    others = m_buf.at[pl.ds(0, n_row - 1)]
    pltpu.make_async_copy(others, others, m_recv).wait()
    m_all = jnp.concatenate([m_buf[q] for q in range(n_row)], axis=0)
    m_high, m_low = split(m_all)
    predicted = dot_bf16(t_parts[...], jnp.concatenate([m_high, m_high], axis=0), (1, 0))
    predicted = predicted + dot_bf16(t_parts[:, :depth], m_low, (1, 0))
    w_ref[...] = l_buf[...] * predicted

    pltpu.make_async_copy(mass_in, mass_in, mass_recv).wait()
    total = jnp.sum(mass + jnp.sum(mass_in[...], axis=0))
    s_ref[...] = jnp.full(s_ref.shape, cells, F32) / total

    pltpu.make_async_copy(g_in, g_in, g_send).wait()
    pltpu.make_async_copy(others, others, m_send).wait()
    pltpu.make_async_copy(mass_in, mass_in, mass_send).wait()


def shards(panel_rows, trans_bias, trans_rate, likelihood):
    n_row, n_col = lax.axis_size("row"), lax.axis_size("col")
    rows, width = panel_rows.shape
    cells = float(likelihood.shape[0] * n_row * likelihood.shape[1] * n_col)
    dma = pltpu.SemaphoreType.DMA
    weighted, scale = pl.pallas_call(
        functools.partial(window_kernel, n_row, n_col, cells),
        out_shape=(
            jax.ShapeDtypeStruct(likelihood.shape, F32),
            jax.ShapeDtypeStruct((1, 128), F32),
        ),
        in_specs=[pl.BlockSpec(memory_space=pltpu.HBM)] * 4,
        out_specs=(
            pl.BlockSpec(memory_space=pltpu.VMEM),
            pl.BlockSpec(memory_space=pltpu.VMEM),
        ),
        scratch_shapes=[
            pltpu.VMEM((rows, width), F32),
            pltpu.VMEM((rows, width), F32),
            pltpu.VMEM(trans_bias.shape, F32),
            pltpu.VMEM((trans_bias.shape[0], 2 * trans_bias.shape[1]), jnp.bfloat16),
            pltpu.VMEM(trans_rate.shape, F32),
            pltpu.VMEM((2,) + trans_rate.shape[::-1], jnp.bfloat16),
            pltpu.VMEM(likelihood.shape, F32),
            pltpu.VMEM((n_row, rows, width), F32),
            pltpu.VMEM((n_row - 1, rows, width), F32),
            pltpu.VMEM((n_row, rows, width), F32),
            pltpu.VMEM((1, 128), F32),
            pltpu.VMEM((n_row * n_col - 1, 1, 128), F32),
            dma((2 + 2 * PIECES,)), dma, dma, dma, dma, dma, dma, dma, dma,
        ],
        compiler_params=pltpu.CompilerParams(collective_id=0, has_side_effects=True, vmem_limit_bytes=24 * 2**20),
        name="window",
    )(*[pltpu.with_memory_space_constraint(x, pltpu.HBM) for x in (panel_rows, trans_bias, trans_rate, likelihood)])
    return weighted * scale[0, 0]


def solution(mesh):
    placed = (P("row", "col"), P("row", None), P("col", None), P("row", "col"))
    return jax.shard_map(
        shards, mesh=mesh, in_specs=placed, out_specs=P("row", "col"), check_vma=False
    )
```

```python
import functools

import jax
import jax.numpy as jnp
from jax import lax
from jax.experimental import pallas as pl
from jax.experimental.pallas import tpu as pltpu
from jax.sharding import PartitionSpec as P

MESH = pl.DeviceIdType.MESH
F32 = jnp.float32
PIECES = 1


def split(x):
    high = x.astype(jnp.bfloat16)
    return high, (x - high.astype(F32)).astype(jnp.bfloat16)


def dot_bf16(a, b, contract):
    return lax.dot_general(
        a, b, ((contract[:1], contract[1:]), ((), ())), preferred_element_type=F32
    )


def wrapped(position, size):
    return jnp.where(position >= size, position - size, position)


def window_kernel(
    n_row, n_col, cells,
    p_hbm, t_hbm, r_hbm, l_hbm,
    w_ref, s_ref,
    p_buf, p_next, t_buf, t_parts, r_buf, r_parts, l_buf, g_out, g_in, m_buf, mass_out, mass_in,
    load_sems, p_send, p_recv, g_send, g_recv, m_send, m_recv, mass_send, mass_recv,
):
    i = lax.axis_index("row")
    j = lax.axis_index("col")
    rows, width = p_buf.shape
    far_first = sorted(range(1, n_row), key=lambda d: abs(2 * d - n_row))
    row_of = [i] + [wrapped(i + d, n_row) for d in range(1, n_row)]
    col_of = [j] + [wrapped(j + d, n_col) for d in range(1, n_col)]
    depth = t_buf.shape[1]
    height = t_buf.shape[0] // PIECES
    pieces = [pl.ds(k * height, height) for k in range(PIECES)]
    p_load = pltpu.make_async_copy(p_hbm, p_buf, load_sems.at[0])
    r_load = pltpu.make_async_copy(r_hbm, r_buf, load_sems.at[1])
    t_loads = [
        pltpu.make_async_copy(t_hbm.at[piece], t_buf.at[piece], load_sems.at[2 + k])
        for k, piece in enumerate(pieces)
    ]
    l_loads = [
        pltpu.make_async_copy(l_hbm.at[piece], l_buf.at[piece], load_sems.at[2 + PIECES + k])
        for k, piece in enumerate(pieces)
    ]
    p_load.start()
    for t_load, l_load in zip(t_loads, l_loads):
        t_load.start()
        l_load.start()
    r_load.start()

    barrier = pltpu.get_barrier_semaphore()
    for d in range(1, n_row):
        pl.semaphore_signal(
            barrier, inc=1, device_id=(row_of[d], j), device_id_type=MESH
        )
    for d in range(1, n_col):
        pl.semaphore_signal(
            barrier, inc=1, device_id=(i, col_of[d]), device_id_type=MESH
        )
    g = None
    for piece, t_load, l_load in zip(pieces, t_loads, l_loads):
        t_load.wait()
        t_high, t_low = split(t_buf[piece])
        t_parts[piece, :depth] = t_high
        t_parts[piece, depth:] = t_low
        l_load.wait()
        l_high, l_low = split(l_buf[piece])
        both = dot_bf16(t_parts[piece], l_high, (0, 0))
        part = both[:depth] + both[depth:] + dot_bf16(t_high, l_low, (0, 0))
        g = part if g is None else g + part
    for q in range(n_row):
        g_out[q] = g[q * rows:(q + 1) * rows]
    p_load.wait()
    r_load.wait()
    r_high, r_low = split(r_buf[...].T)
    r_parts[0] = r_high
    r_parts[1] = r_low

    def rate_rows(p_rows, start):
        p_high, p_low = split(p_rows)
        high = r_parts[0, start:start + width]
        low = r_parts[1, start:start + width]
        return (
            dot_bf16(p_high, low, (1, 0)) + dot_bf16(p_low, high, (1, 0))
            + dot_bf16(p_high, high, (1, 0))
        )

    m = rate_rows(p_buf[...], 0)
    pl.semaphore_wait(barrier, n_row - 1 + n_col - 1)

    next_copy = pltpu.make_async_remote_copy(
        src_ref=p_buf, dst_ref=p_next, send_sem=p_send, recv_sem=p_recv,
        device_id=(i, col_of[n_col - 1]), device_id_type=MESH,
    )
    next_copy.start()

    for d in far_first:
        peer = row_of[d]
        pltpu.make_async_remote_copy(
            src_ref=g_out.at[peer], dst_ref=g_in.at[d - 1],
            send_sem=g_send, recv_sem=g_recv,
            device_id=(peer, j), device_id_type=MESH,
        ).start()

    next_copy.wait()
    m = m + rate_rows(p_next[...], width)
    m_buf[i] = m
    for d in far_first:
        pltpu.make_async_remote_copy(
            src_ref=m_buf.at[i], dst_ref=m_buf.at[i],
            send_sem=m_send, recv_sem=m_recv,
            device_id=(row_of[d], j), device_id_type=MESH,
        ).start()

    pltpu.make_async_copy(g_in, g_in, g_recv).wait()
    g_sum = g_out[i]
    for d in range(1, n_row):
        g_sum = g_sum + g_in[d - 1]
    mass = jnp.sum(g_sum * m, axis=0, keepdims=True)
    mass = sum(mass[:, k:k + 128] for k in range(0, width, 128))
    mass_out[...] = mass

    def send_mass(row, first, from_col):
        for d in range(from_col, n_col):
            pltpu.make_async_remote_copy(
                src_ref=mass_out, dst_ref=mass_in.at[first + d - 1],
                send_sem=mass_send, recv_sem=mass_recv,
                device_id=(row, col_of[d]), device_id_type=MESH,
            ).start()

    if n_row * n_col <= 64:
        for d in reversed(range(1, n_row)):
            send_mass(row_of[d], d * n_col, 0)
    else:

        def send_row(d, carry):
            send_mass(wrapped(i + d, n_row), d * n_col, 0)
            return carry

        lax.fori_loop(1, n_row, send_row, 0)
    send_mass(i, 0, 1)

    others = m_buf.at[pl.ds(0, n_row - 1)]
    pltpu.make_async_copy(others, others, m_recv).wait()
    m_all = jnp.concatenate([m_buf[q] for q in range(n_row)], axis=0)
    m_high, m_low = split(m_all)
    predicted = dot_bf16(t_parts[...], jnp.concatenate([m_high, m_high], axis=0), (1, 0))
    predicted = predicted + dot_bf16(t_parts[:, :depth], m_low, (1, 0))
    w_ref[...] = l_buf[...] * predicted

    pltpu.make_async_copy(mass_in, mass_in, mass_recv).wait()
    total = jnp.sum(mass + jnp.sum(mass_in[...], axis=0))
    s_ref[...] = jnp.full(s_ref.shape, cells, F32) / total

    pltpu.make_async_copy(g_in, g_in, g_send).wait()
    pltpu.make_async_copy(others, others, m_send).wait()
    pltpu.make_async_copy(mass_in, mass_in, mass_send).wait()


def shards(panel_rows, trans_bias, trans_rate, likelihood):
    n_row, n_col = lax.axis_size("row"), lax.axis_size("col")
    rows, width = panel_rows.shape
    cells = float(likelihood.shape[0] * n_row * likelihood.shape[1] * n_col)
    dma = pltpu.SemaphoreType.DMA
    weighted, scale = pl.pallas_call(
        functools.partial(window_kernel, n_row, n_col, cells),
        out_shape=(
            jax.ShapeDtypeStruct(likelihood.shape, F32),
            jax.ShapeDtypeStruct((1, 128), F32),
        ),
        in_specs=[pl.BlockSpec(memory_space=pltpu.HBM)] * 4,
        out_specs=(
            pl.BlockSpec(memory_space=pltpu.VMEM),
            pl.BlockSpec(memory_space=pltpu.VMEM),
        ),
        scratch_shapes=[
            pltpu.VMEM((rows, width), F32),
            pltpu.VMEM((rows, width), F32),
            pltpu.VMEM(trans_bias.shape, F32),
            pltpu.VMEM((trans_bias.shape[0], 2 * trans_bias.shape[1]), jnp.bfloat16),
            pltpu.VMEM(trans_rate.shape, F32),
            pltpu.VMEM((2,) + trans_rate.shape[::-1], jnp.bfloat16),
            pltpu.VMEM(likelihood.shape, F32),
            pltpu.VMEM((n_row, rows, width), F32),
            pltpu.VMEM((n_row - 1, rows, width), F32),
            pltpu.VMEM((n_row, rows, width), F32),
            pltpu.VMEM((1, 128), F32),
            pltpu.VMEM((n_row * n_col - 1, 1, 128), F32),
            dma((2 + 2 * PIECES,)), dma, dma, dma, dma, dma, dma, dma, dma,
        ],
        compiler_params=pltpu.CompilerParams(collective_id=0, has_side_effects=True, vmem_limit_bytes=24 * 2**20),
        name="window",
    )(*[pltpu.with_memory_space_constraint(x, pltpu.HBM) for x in (panel_rows, trans_bias, trans_rate, likelihood)])
    return weighted * scale[0, 0]


def solution(mesh):
    placed = (P("row", "col"), P("row", None), P("col", None), P("row", "col"))
    return jax.shard_map(
        shards, mesh=mesh, in_specs=placed, out_specs=P("row", "col"), check_vma=False
    )
```
